32 devices in a mesh: pop: 16 (over z, x, core), tp: 2 (over y).
Axes of the slice: x: 2, y: 2, z: 4, core: 2. Of those that a mesh axis runs over, the one named last changes fastest.
Arguments:
- tokens: bfloat16 [6144, 3584], P(('pop', 'tp')), may hold values from -6 to 6
- norm_gain: bfloat16 [3584], replicated, may hold values from 0.5 to 1.5
- weight: bfloat16 [3584, 10240], P('pop', 'tp'), may hold values from -0.09375 to 0.09375
- pair_seeds: int32 [32], P('pop'), may hold values from 0 to 1073741823
- member_ranks: int32 [64], P('pop'), may hold values from 0 to 63, each once
Outputs:
- activated: bfloat16 [6144, 10240], P('pop', 'tp')
- estimate: float32 [3584, 10240], P('pop', 'tp')
The draws below stay inside these ranges and needn't reach their ends.
Inputs may be any that keep to these rules, and one draw needn't show every extreme that they name: `member_ranks`: each of 0 to 63 appears once.
All inputs are finite; a program needn't handle non-finite values.
Results may differ from the reference program's by a relative error of at most 0.0051.
Values may be sent and summed in bfloat16 or wider, within the bound.
A program may use at most 128 MiB of HBM per device.

```python
import jax
import jax.numpy as jnp
from jax import lax

D = 3584
FFW = 10240
ROWS = 96
PAIRS = 32
MEMBERS = 64


def plant(values, rng, low, high):
    shape = values.shape
    index_at = [jax.random.randint(jax.random.fold_in(rng, axis), (), 0, shape[axis]) for axis in range(len(shape))]
    values = values.at[tuple(index_at)].set(low)
    longest = shape.index(max(shape))
    index_at[longest] = (index_at[longest] + 1) % shape[longest]
    return values.at[tuple(index_at)].set(high)


def steps_of(stream_key, dims, shards, least, high):
    loudness = 1.0
    for dim, shards_of in shards:
        steps = jax.random.uniform(jax.random.fold_in(jax.random.fold_in(stream_key, 6), dim), (shards_of,), jnp.float32, least / len(shards), high / len(shards))
        loudness = loudness * jnp.repeat(jnp.exp(steps), dims[dim] // shards_of).reshape((-1,) + (1,) * (len(dims) - 1 - dim))
    return loudness


def normal_values(stream_key, extent, width, bound, shards=(), kind=jnp.bfloat16):
    entries = jax.random.normal(stream_key, extent, jnp.float32) * width
    if len(shards) > 0:
        entries = steps_of(stream_key, extent, shards, -0.22, 0.18) * entries
    return jnp.clip(entries, min=-bound, max=bound).astype(kind)


def setup_inputs(seed: int = 0) -> dict:
    keys = jax.random.split(jax.random.key(seed), 6)
    tokens = normal_values(keys[0], (MEMBERS * ROWS, D), 1.0, 6.0, ((0, 32),))
    norm_gain = jnp.clip(1.0 + 0.1 * jax.random.normal(keys[1], (D,), jnp.float32), 0.5, 1.5).astype(jnp.bfloat16)
    weight = normal_values(keys[2], (D, FFW), D ** -0.5, 0.09375, ((0, 16), (1, 2)))
    pair_seeds = plant(jax.random.randint(keys[3], (PAIRS,), 0, 1073741824), jax.random.fold_in(keys[3], 1), 0, 1073741823).astype(jnp.int32)
    member_ranks = jax.random.permutation(keys[4], MEMBERS).astype(jnp.int32)
    return {"tokens": tokens, "norm_gain": norm_gain, "weight": weight, "pair_seeds": pair_seeds, "member_ranks": member_ranks}


noise_scale = 0.01
mix_seed = -1640531535
mix_first = -2048144789
mix_second = -1028477387

def shifted(values, amount):
    return lax.shift_right_logical(values, jnp.full_like(values, amount))

def noise_block(seed_value, row_ids, col_ids):
    counter = row_ids[:, None] * jnp.int32(FFW) + col_ids[None, :]
    hashed = seed_value * jnp.int32(mix_seed) + counter
    hashed = hashed ^ shifted(hashed, 16)
    hashed = hashed * jnp.int32(mix_first)
    hashed = hashed ^ shifted(hashed, 13)
    hashed = hashed * jnp.int32(mix_second)
    hashed = hashed ^ shifted(hashed, 16)
    lower = hashed & 255
    upper = shifted(hashed, 8) & 255
    return (lower + upper - 255).astype(jnp.float32) / 128.0

def normalize(tokens, norm_gain):
    values = tokens.astype(jnp.float32)
    factor = lax.rsqrt(lax.optimization_barrier(jnp.mean(values * values, axis=1, keepdims=True)) + 1e-06)
    return (values * factor * norm_gain.astype(jnp.float32)).astype(jnp.bfloat16)

def reference(tokens, norm_gain, weight, pair_seeds, member_ranks):
    normed = normalize(tokens, norm_gain)
    base_sum = jnp.dot(normed, weight, preferred_element_type=jnp.float32)
    members = member_ranks.shape[0]
    pairs = pair_seeds.shape[0]
    row_ids = jnp.arange(D, dtype=jnp.int32)
    col_ids = jnp.arange(FFW, dtype=jnp.int32)
    signed = jnp.concatenate([jnp.ones((ROWS, 1), jnp.float32), -jnp.ones((ROWS, 1), jnp.float32)], 0)
    pair_tokens = normed.reshape(pairs, 2 * ROWS, D)
    coefs = (member_ranks[0::2] - member_ranks[1::2]).astype(jnp.float32) / ((members - 1) * members * noise_scale)

    def advance(running, bundle):
        seed_value, pair_rows, weight_coef = bundle
        sample = noise_block(seed_value, row_ids, col_ids)
        product = jnp.dot(pair_rows, sample.astype(jnp.bfloat16), preferred_element_type=jnp.float32)
        return (running + weight_coef * sample, product)
    estimate, products = lax.scan(advance, jnp.zeros((D, FFW), jnp.float32), (pair_seeds, pair_tokens, coefs))
    noise_terms = (products * signed[None]).reshape(members * ROWS, FFW)
    activated = jax.nn.silu(base_sum + noise_scale * noise_terms).astype(jnp.bfloat16)
    return (activated, estimate)
```

```python
import functools

import jax
import jax.numpy as jnp
from jax import lax
from jax.experimental import pallas as pl
from jax.experimental.pallas import tpu as pltpu
from jax.sharding import PartitionSpec as P

FFW = 10240
ROWS = 96
CHUNKS = 2

noise_scale = 0.01
mix_seed = -1640531535
mix_first = -2048144789
mix_second = -1028477387


def byte_sum(hashed):
    hashed = hashed ^ lax.shift_right_logical(hashed, 16)
    hashed = hashed * jnp.int32(mix_first)
    hashed = hashed ^ lax.shift_right_logical(hashed, 13)
    hashed = hashed * jnp.int32(mix_second)
    hashed = hashed ^ lax.shift_right_logical(hashed, 16)
    low = hashed.astype(jnp.int16)
    return (low & jnp.int16(255)) + lax.shift_right_logical(low, jnp.int16(8))


def counters(height, width):
    rows = lax.broadcasted_iota(jnp.int32, (height, width), 0)
    return rows * FFW + lax.broadcasted_iota(jnp.int32, (height, width), 1)


def pick(extent, options):
    for option in options:
        if extent % option == 0:
            return option
    return extent


def cost(microseconds):
    return pl.CostEstimate(
        flops=int(microseconds * 1.0e9), bytes_accessed=1 << 20, transcendentals=0
    )


def normalize(tokens, norm_gain):
    values = tokens.astype(jnp.float32)
    factor = lax.rsqrt(jnp.mean(values * values, axis=1, keepdims=True) + 1e-06)
    return (values * factor * norm_gain.astype(jnp.float32)).astype(jnp.bfloat16)


def term_kernel(tile, start_ref, rows_ref, out_ref, first, second):
    slots = (first, second)
    height, width = tile
    steps = rows_ref.shape[1] // height
    origin = start_ref[0] + pl.program_id(0) * width
    grid_ids = counters(height, width)

    def fill(step, slot):
        total = byte_sum(grid_ids + (origin + step * height * FFW))
        slot[...] = (total - jnp.int16(255)).astype(jnp.bfloat16)

    fill(0, slots[0])
    for step in range(steps):
        product = jnp.dot(
            rows_ref[:, step * height : (step + 1) * height],
            slots[step % 2][...],
            preferred_element_type=jnp.float32,
        )
        if step + 1 < steps:
            fill(step + 1, slots[(step + 1) % 2])
        if step == 0:
            out_ref[...] = product
        else:
            out_ref[...] += product


def noise_term(start, rows, width):
    tile = (256, pick(width, (512, 256, 128)))
    count, depth = rows.shape
    return pl.pallas_call(
        functools.partial(term_kernel, tile),
        out_shape=jax.ShapeDtypeStruct((count, width), jnp.float32),
        grid=(width // tile[1],),
        in_specs=[
            pl.BlockSpec(memory_space=pltpu.SMEM),
            pl.BlockSpec((count, depth), lambda j: (0, 0)),
        ],
        out_specs=pl.BlockSpec((count, tile[1]), lambda j: (0, j)),
        scratch_shapes=[pltpu.VMEM(tile, jnp.bfloat16)] * 2,
        compiler_params=pltpu.CompilerParams(vmem_limit_bytes=32 << 20),
        cost_estimate=cost(42),
        name="noise_term",
    )(start, rows)


def estimate_kernel(tile, denominator, starts_ref, ranks_ref, out_ref):
    height, width = tile
    pairs = starts_ref.shape[0]
    column = pl.program_id(0) * out_ref.shape[1]
    across = out_ref.shape[1] // width
    grid_ids = counters(height, width)
    rank_total = lax.fori_loop(0, pairs, lambda p, t: t + ranks_ref[p], jnp.int32(0))

    def one(index, carry):
        row = pl.multiple_of(index // across * height, height)
        lane = pl.multiple_of(index % across * width, width)
        ids = grid_ids + (column + row * FFW + lane)

        def add(pair, total):
            part = byte_sum(ids + starts_ref[pair]).astype(jnp.int32)
            return total + ranks_ref[pair] * part

        total = lax.fori_loop(0, pairs, add, jnp.zeros(tile, jnp.int32), unroll=32)
        centred = (total - 255 * rank_total).astype(jnp.float32)
        out_ref[pl.ds(row, height), pl.ds(lane, width)] = centred * (1.0 / denominator)
        return carry

    lax.fori_loop(0, out_ref.shape[0] // height * across, one, 0)


def make_estimate(starts, ranks, rows, width, members):
    block = pick(width, (512, 256, 128))
    tile = (pick(rows, (32, 8)), pick(block, (256, 128)))
    return pl.pallas_call(
        functools.partial(estimate_kernel, tile, 128 * (members - 1) * members * noise_scale),
        out_shape=jax.ShapeDtypeStruct((rows, width), jnp.float32),
        grid=(width // block,),
        in_specs=[pl.BlockSpec(memory_space=pltpu.SMEM)] * 2,
        out_specs=pl.BlockSpec((rows, block), lambda j: (0, j)),
        compiler_params=pltpu.CompilerParams(vmem_limit_bytes=32 << 20),
        cost_estimate=cost(75),
        name="estimate",
    )(starts, ranks)


def project_kernel(spans, offsets_ref, rows_ref, weight_ref, *refs):
    terms, out_ref = refs[:spans], refs[-1]
    base = jnp.dot(rows_ref[...], weight_ref[...], preferred_element_type=jnp.float32)
    span = terms[0].shape[0]
    for index in range(spans):
        for half in range(span // ROWS):
            low = half * ROWS
            scale = (noise_scale / 128) * (1 - 2 * (half % 2))
            value = base[index * span + low : index * span + low + ROWS]
            value = value + scale * terms[index][low : low + ROWS, :]
            value = value / (1.0 + jnp.exp(-value))
            place = pl.multiple_of(offsets_ref[index] + low, 16)
            out_ref[pl.ds(place, ROWS), :] = value.astype(jnp.bfloat16)


def project(offsets, rows, weight, terms, previous, chunk, width):
    count, depth = rows.shape
    part = weight.shape[1]
    block = pick(part, (512, 256, 128))
    first = chunk * (part // block)
    span = terms[0].shape[0]
    operands = [offsets, rows, weight, *terms]
    in_specs = [
        pl.BlockSpec(memory_space=pltpu.SMEM),
        pl.BlockSpec((count, depth), lambda j: (0, 0)),
        pl.BlockSpec((depth, block), lambda j: (0, j)),
    ] + [pl.BlockSpec((span, block), lambda j: (0, j + first))] * len(terms)
    aliases = {}
    if previous is not None:
        aliases = {len(operands): 0}
        operands.append(previous)
        in_specs.append(pl.BlockSpec(memory_space=pl.ANY))
    return pl.pallas_call(
        functools.partial(project_kernel, len(terms)),
        out_shape=jax.ShapeDtypeStruct((count, width), jnp.bfloat16),
        grid=(part // block,),
        in_specs=in_specs,
        out_specs=pl.BlockSpec((count, block), lambda j: (0, j + first)),
        input_output_aliases=aliases,
        compiler_params=pltpu.CompilerParams(vmem_limit_bytes=48 << 20),
        cost_estimate=cost(16 / CHUNKS),
        name="project",
    )(*operands)


def collect(values, axis, size):
    if size & (size - 1):
        return lax.all_gather(values, axis, axis=0, tiled=False)
    place = lax.axis_index(axis)
    block = values[None]
    step = 1
    while step < size:
        other = lax.ppermute(block, axis, [(i, i ^ step) for i in range(size)])
        upper = (place & step) != 0
        block = jnp.concatenate(
            [jnp.where(upper, other, block), jnp.where(upper, block, other)], 0
        )
        step *= 2
    return block


def shards(pops, tps, tokens, norm_gain, weight, pair_seeds, member_ranks):
    owned_rows, width = weight.shape
    pop_index, tp_index = lax.axis_index("pop"), lax.axis_index("tp")
    part = width // CHUNKS
    gathered = [
        lax.all_gather(weight[:, c * part : (c + 1) * part], "pop", axis=0, tiled=True)
        for c in range(CHUNKS)
    ]
    pairs = pair_seeds.shape[0]
    col_start = tp_index * width
    starts = pair_seeds * jnp.int32(mix_seed) + col_start

    span = 2 * ROWS
    if tps == pairs and tokens.shape[0] == span:
        order = [(tp_index + step) % tps for step in range(tps)]
        pieces = [tokens]
        for step in range(1, tps):
            shift = [((i + step) % tps, i) for i in range(tps)]
            pieces.append(lax.ppermute(tokens, "tp", shift))
        pieces = [normalize(piece, norm_gain) for piece in pieces]
    else:
        order = [jnp.int32(step) for step in range(pairs)]
        normed = normalize(lax.all_gather(tokens, "tp", axis=0, tiled=True), norm_gain)
        pieces = [normed[i * span : (i + 1) * span] for i in range(pairs)]
    terms = [
        noise_term(lax.dynamic_slice(starts, (place,), (1,)), piece, width)
        for place, piece in zip(order, pieces)
    ]

    everyone = collect(jnp.concatenate([pair_seeds, member_ranks]), "pop", pops)
    all_seeds = everyone[:, :pairs].reshape(-1)
    all_ranks = everyone[:, pairs:].reshape(-1)
    estimate = make_estimate(
        all_seeds * jnp.int32(mix_seed) + pop_index * (owned_rows * FFW) + col_start,
        all_ranks[0::2] - all_ranks[1::2],
        owned_rows,
        width,
        all_ranks.shape[0],
    )

    offsets = jnp.stack([place * span for place in order]).astype(jnp.int32)
    normed = jnp.concatenate(pieces, 0)
    activated = None
    for chunk in range(CHUNKS):
        activated = project(offsets, normed, gathered[chunk], terms, activated, chunk, width)
    return (activated, estimate)


def solution(mesh):
    placed = (P(("pop", "tp"), None), P(), P("pop", "tp"), P("pop"), P("pop"))
    return jax.shard_map(
        functools.partial(shards, mesh.shape["pop"], mesh.shape["tp"]),
        mesh=mesh,
        in_specs=placed,
        out_specs=(P("pop", "tp"), P("pop", "tp")),
        check_vma=False,
    )
```

```python
import functools
import math

import jax
import jax.numpy as jnp
from jax import lax
from jax.experimental import pallas as pl
from jax.experimental.pallas import tpu as pltpu
from jax.sharding import PartitionSpec as P

FFW = 10240
ROWS = 96

noise_scale = 0.01
mix_seed = -1640531535
mix_first = -2048144789
mix_second = -1028477387


def byte_sum(hashed):
    hashed = hashed ^ lax.shift_right_logical(hashed, 16)
    hashed = hashed * jnp.int32(mix_first)
    hashed = hashed ^ lax.shift_right_logical(hashed, 13)
    hashed = hashed * jnp.int32(mix_second)
    hashed = hashed ^ lax.shift_right_logical(hashed, 16)
    low = hashed.astype(jnp.int16)
    return (low & jnp.int16(255)) + lax.shift_right_logical(low, jnp.int16(8))


def counters(height, width):
    rows = lax.broadcasted_iota(jnp.int32, (height, width), 0)
    return rows * FFW + lax.broadcasted_iota(jnp.int32, (height, width), 1)


def pick(extent, options):
    for option in options:
        if extent % option == 0:
            return option
    return extent


def cost(microseconds):
    return pl.CostEstimate(
        flops=int(microseconds * 1.0e9), bytes_accessed=1 << 20, transcendentals=0
    )


def normalize(tokens, norm_gain):
    values = tokens.astype(jnp.float32)
    factor = lax.rsqrt(jnp.mean(values * values, axis=1, keepdims=True) + 1e-06)
    return (values * factor * norm_gain.astype(jnp.float32)).astype(jnp.bfloat16)


def term_kernel(tile, start_ref, rows_ref, out_ref, first, second):
    slots = (first, second)
    height, width = tile
    steps = rows_ref.shape[1] // height
    origin = start_ref[0] + pl.program_id(0) * width
    grid_ids = counters(height, width)

    def fill(step, slot):
        total = byte_sum(grid_ids + (origin + step * height * FFW))
        slot[...] = (total - jnp.int16(255)).astype(jnp.bfloat16)

    fill(0, slots[0])
    for step in range(steps):
        product = jnp.dot(
            rows_ref[:, step * height : (step + 1) * height],
            slots[step % 2][...],
            preferred_element_type=jnp.float32,
        )
        if step + 1 < steps:
            fill(step + 1, slots[(step + 1) % 2])
        if step == 0:
            out_ref[...] = product
        else:
            out_ref[...] += product


def noise_term(start, rows, width):
    tile = (256, pick(width, (512, 256, 128)))
    count, depth = rows.shape
    return pl.pallas_call(
        functools.partial(term_kernel, tile),
        out_shape=jax.ShapeDtypeStruct((count, width), jnp.float32),
        grid=(width // tile[1],),
        in_specs=[
            pl.BlockSpec(memory_space=pltpu.SMEM),
            pl.BlockSpec((count, depth), lambda j: (0, 0)),
        ],
        out_specs=pl.BlockSpec((count, tile[1]), lambda j: (0, j)),
        scratch_shapes=[pltpu.VMEM(tile, jnp.bfloat16)] * 2,
        compiler_params=pltpu.CompilerParams(vmem_limit_bytes=56 << 20),
        cost_estimate=cost(42),
        name="noise_term",
    )(start, rows)


def estimate_kernel(tile, denominator, starts_ref, ranks_ref, out_ref):
    height, width = tile
    pairs = starts_ref.shape[0]
    column = pl.program_id(0) * out_ref.shape[1]
    across = out_ref.shape[1] // width
    grid_ids = counters(height, width)
    rank_total = lax.fori_loop(0, pairs, lambda p, t: t + ranks_ref[p], jnp.int32(0))

    def one(index, carry):
        row = pl.multiple_of(index // across * height, height)
        lane = pl.multiple_of(index % across * width, width)
        ids = grid_ids + (column + row * FFW + lane)

        def add(pair, total):
            part = byte_sum(ids + starts_ref[pair]).astype(jnp.int32)
            return total + ranks_ref[pair] * part

        total = lax.fori_loop(0, pairs, add, jnp.zeros(tile, jnp.int32), unroll=32)
        centred = (total - 255 * rank_total).astype(jnp.float32)
        out_ref[pl.ds(row, height), pl.ds(lane, width)] = centred * (1.0 / denominator)
        return carry

    lax.fori_loop(0, out_ref.shape[0] // height * across, one, 0)


def make_estimate(starts, ranks, rows, width, members):
    block = pick(width, (512, 256, 128))
    tile = (pick(rows, (32, 8)), pick(block, (256, 128)))
    return pl.pallas_call(
        functools.partial(estimate_kernel, tile, 128 * (members - 1) * members * noise_scale),
        out_shape=jax.ShapeDtypeStruct((rows, width), jnp.float32),
        grid=(width // block,),
        in_specs=[pl.BlockSpec(memory_space=pltpu.SMEM)] * 2,
        out_specs=pl.BlockSpec((rows, block), lambda j: (0, j)),
        compiler_params=pltpu.CompilerParams(vmem_limit_bytes=56 << 20),
        cost_estimate=cost(75),
        name="estimate",
    )(starts, ranks)


def project_kernel(spans, offsets_ref, rows_ref, weight_ref, *refs):
    terms, out_ref = refs[:spans], refs[-1]
    base = jnp.dot(rows_ref[...], weight_ref[...], preferred_element_type=jnp.float32)
    span = terms[0].shape[0]
    for index in range(spans):
        for half in range(span // ROWS):
            low = half * ROWS
            scale = (noise_scale / 128) * (1 - 2 * (half % 2))
            value = base[index * span + low : index * span + low + ROWS]
            value = value + scale * terms[index][low : low + ROWS, :]
            value = value / (1.0 + jnp.exp(-value))
            place = pl.multiple_of(offsets_ref[index] + low, 16)
            out_ref[pl.ds(place, ROWS), :] = value.astype(jnp.bfloat16)


def project(offsets, rows, weight, terms, previous, column, width):
    count, depth = rows.shape
    part = weight.shape[1]
    block = pick(math.gcd(part, column), (512, 256, 128) if column == 0 else (256, 128))
    first = column // block
    span = terms[0].shape[0]
    operands = [offsets, rows, weight, *terms]
    in_specs = [
        pl.BlockSpec(memory_space=pltpu.SMEM),
        pl.BlockSpec((count, depth), lambda j: (0, 0)),
        pl.BlockSpec((depth, block), lambda j: (0, j)),
    ] + [pl.BlockSpec((span, block), lambda j: (0, j + first))] * len(terms)
    aliases = {}
    if previous is not None:
        aliases = {len(operands): 0}
        operands.append(previous)
        in_specs.append(pl.BlockSpec(memory_space=pl.ANY))
    return pl.pallas_call(
        functools.partial(project_kernel, len(terms)),
        out_shape=jax.ShapeDtypeStruct((count, width), jnp.bfloat16),
        grid=(part // block,),
        in_specs=in_specs,
        out_specs=pl.BlockSpec((count, block), lambda j: (0, j + first)),
        input_output_aliases=aliases,
        compiler_params=pltpu.CompilerParams(vmem_limit_bytes=56 << 20),
        cost_estimate=cost(part / 200),
        name="project",
    )(*operands)


def spread(held, digit):
    ordered = []
    for value in range(len(held)):
        piece = held[0]
        for k in range(1, len(held)):
            piece = jnp.where((digit ^ k) == value, held[k], piece)
        ordered.append(piece)
    return jnp.concatenate(ordered, 0)


def collect(values, axis, size, anchors):
    if size & (size - 1):
        return lax.all_gather(values, axis, axis=0, tiled=False), anchors
    block, step, stage, anchors = values[None], 1, 0, list(anchors)
    while step < size:
        radix = 4 if size // step >= 4 else 2
        held = [block] + [
            lax.ppermute(block, axis, [(i, i ^ (k * step)) for i in range(size)])
            for k in range(1, radix)
        ]
        if stage < len(anchors):
            held, anchors[stage] = lax.optimization_barrier((held, anchors[stage]))
        block = spread(held, lax.axis_index(axis) // step % radix)
        step *= radix
        stage += 1
    return block, anchors


def shards(pops, tps, tokens, norm_gain, weight, pair_seeds, member_ranks):
    owned_rows, width = weight.shape
    pop_index, tp_index = lax.axis_index("pop"), lax.axis_index("tp")
    split = width * 4 // 5 // 128 * 128
    gathered = [
        lax.all_gather(weight[:, :split], "pop", axis=0, tiled=True),
        lax.all_gather(weight[:, split:], "pop", axis=0, tiled=True),
    ]
    pairs = pair_seeds.shape[0]
    col_start = tp_index * width
    starts = pair_seeds * jnp.int32(mix_seed) + col_start

    span = 2 * ROWS
    if tps == pairs and tokens.shape[0] == span:
        order = [(tp_index + step) % tps for step in range(tps)]
        arrived = [tokens] + [
            lax.ppermute(tokens, "tp", [((i + step) % tps, i) for i in range(tps)])
            for step in range(1, tps)
        ]
    else:
        order = [jnp.int32(step) for step in range(pairs)]
        whole = lax.all_gather(tokens, "tp", axis=0, tiled=True)
        arrived = [whole[i * span : (i + 1) * span] for i in range(pairs)]
    pieces, terms = [], []
    for place, piece in zip(order, arrived):
        if terms:
            piece, terms[-1] = lax.optimization_barrier((piece, terms[-1]))
        pieces.append(normalize(piece, norm_gain))
        start = lax.dynamic_slice(starts, (place,), (1,))
        terms.append(noise_term(start, pieces[-1], width))

    everyone, terms = collect(jnp.concatenate([pair_seeds, member_ranks]), "pop", pops, terms)
    everyone, terms = lax.optimization_barrier((everyone, terms))
    all_seeds = everyone[:, :pairs].reshape(-1)
    all_ranks = everyone[:, pairs:].reshape(-1)
    estimate = make_estimate(
        all_seeds * jnp.int32(mix_seed) + pop_index * (owned_rows * FFW) + col_start,
        all_ranks[0::2] - all_ranks[1::2],
        owned_rows,
        width,
        all_ranks.shape[0],
    )

    offsets = jnp.stack([place * span for place in order]).astype(jnp.int32)
    normed = jnp.concatenate(pieces, 0)
    terms, estimate = lax.optimization_barrier((terms, estimate))
    activated, first = None, 0
    for piece in gathered:
        activated = project(offsets, normed, piece, terms, activated, first, width)
        first += piece.shape[1]
    return (activated, estimate)


def solution(mesh):
    placed = (P(("pop", "tp"), None), P(), P("pop", "tp"), P("pop"), P("pop"))
    return jax.shard_map(
        functools.partial(shards, mesh.shape["pop"], mesh.shape["tp"]),
        mesh=mesh,
        in_specs=placed,
        out_specs=(P("pop", "tp"), P("pop", "tp")),
        check_vma=False,
    )
```

```python
import functools

import jax
import jax.numpy as jnp
from jax import lax
from jax.experimental import pallas as pl
from jax.experimental.pallas import tpu as pltpu
from jax.sharding import PartitionSpec as P

FFW = 10240
ROWS = 96

noise_scale = 0.01
mix_seed = -1640531535
mix_first = -2048144789
mix_second = -1028477387


def byte_sum(hashed):
    hashed = hashed ^ lax.shift_right_logical(hashed, 16)
    hashed = hashed * jnp.int32(mix_first)
    hashed = hashed ^ lax.shift_right_logical(hashed, 13)
    hashed = hashed * jnp.int32(mix_second)
    hashed = hashed ^ lax.shift_right_logical(hashed, 16)
    low = hashed.astype(jnp.int16)
    return (low & jnp.int16(255)) + lax.shift_right_logical(low, jnp.int16(8))


def counters(height, width):
    rows = lax.broadcasted_iota(jnp.int32, (height, width), 0)
    return rows * FFW + lax.broadcasted_iota(jnp.int32, (height, width), 1)


def pick(extent, options):
    for option in options:
        if extent % option == 0:
            return option
    return extent


def cost(microseconds):
    return pl.CostEstimate(
        flops=int(microseconds * 1.0e9), bytes_accessed=1 << 20, transcendentals=0
    )


def normalize(tokens, norm_gain):
    values = tokens.astype(jnp.float32)
    factor = lax.rsqrt(jnp.mean(values * values, axis=1, keepdims=True) + 1e-06)
    return (values * factor * norm_gain.astype(jnp.float32)).astype(jnp.bfloat16)


def term_kernel(tile, start_ref, rows_ref, out_ref, first, second):
    slots = (first, second)
    height, width = tile
    steps = rows_ref.shape[1] // height
    origin = start_ref[0] + pl.program_id(0) * width
    grid_ids = counters(height, width)

    def fill(step, slot):
        total = byte_sum(grid_ids + (origin + step * height * FFW))
        slot[...] = (total - jnp.int16(255)).astype(jnp.bfloat16)

    fill(0, slots[0])
    for step in range(steps):
        product = jnp.dot(
            rows_ref[:, step * height : (step + 1) * height],
            slots[step % 2][...],
            preferred_element_type=jnp.float32,
        )
        if step + 1 < steps:
            fill(step + 1, slots[(step + 1) % 2])
        if step == 0:
            out_ref[...] = product
        else:
            out_ref[...] += product


def noise_term(start, rows, width):
    tile = (256, pick(width, (512, 256, 128)))
    count, depth = rows.shape
    return pl.pallas_call(
        functools.partial(term_kernel, tile),
        out_shape=jax.ShapeDtypeStruct((count, width), jnp.float32),
        grid=(width // tile[1],),
        in_specs=[
            pl.BlockSpec(memory_space=pltpu.SMEM),
            pl.BlockSpec((count, depth), lambda j: (0, 0)),
        ],
        out_specs=pl.BlockSpec((count, tile[1]), lambda j: (0, j)),
        scratch_shapes=[pltpu.VMEM(tile, jnp.bfloat16)] * 2,
        compiler_params=pltpu.CompilerParams(vmem_limit_bytes=56 << 20),
        cost_estimate=cost(42),
        name="noise_term",
    )(start, rows)


def estimate_kernel(tile, denominator, starts_ref, ranks_ref, out_ref):
    height, width = tile
    pairs = starts_ref.shape[0]
    column = pl.program_id(0) * out_ref.shape[1]
    across = out_ref.shape[1] // width
    grid_ids = counters(height, width)
    rank_total = lax.fori_loop(0, pairs, lambda p, t: t + ranks_ref[p], jnp.int32(0))

    def one(index, carry):
        row = pl.multiple_of(index // across * height, height)
        lane = pl.multiple_of(index % across * width, width)
        ids = grid_ids + (column + row * FFW + lane)

        def add(pair, total):
            part = byte_sum(ids + starts_ref[pair]).astype(jnp.int32)
            return total + ranks_ref[pair] * part

        total = lax.fori_loop(0, pairs, add, jnp.zeros(tile, jnp.int32), unroll=32)
        centred = (total - 255 * rank_total).astype(jnp.float32)
        out_ref[pl.ds(row, height), pl.ds(lane, width)] = centred * (1.0 / denominator)
        return carry

    lax.fori_loop(0, out_ref.shape[0] // height * across, one, 0)


def make_estimate(starts, ranks, rows, width, members):
    block = pick(width, (512, 256, 128))
    tile = (pick(rows, (32, 8)), pick(block, (256, 128)))
    return pl.pallas_call(
        functools.partial(estimate_kernel, tile, 128 * (members - 1) * members * noise_scale),
        out_shape=jax.ShapeDtypeStruct((rows, width), jnp.float32),
        grid=(width // block,),
        in_specs=[pl.BlockSpec(memory_space=pltpu.SMEM)] * 2,
        out_specs=pl.BlockSpec((rows, block), lambda j: (0, j)),
        compiler_params=pltpu.CompilerParams(vmem_limit_bytes=56 << 20),
        cost_estimate=cost(75),
        name="estimate",
    )(starts, ranks)


def project_kernel(spans, offsets_ref, rows_ref, weight_ref, *refs):
    terms, out_ref = refs[:spans], refs[-1]
    base = jnp.dot(rows_ref[...], weight_ref[...], preferred_element_type=jnp.float32)
    span = terms[0].shape[0]
    for index in range(spans):
        for half in range(span // ROWS):
            low = half * ROWS
            scale = (noise_scale / 128) * (1 - 2 * (half % 2))
            value = base[index * span + low : index * span + low + ROWS]
            value = value + scale * terms[index][low : low + ROWS, :]
            value = value / (1.0 + jnp.exp(-value))
            place = pl.multiple_of(offsets_ref[index] + low, 16)
            out_ref[pl.ds(place, ROWS), :] = value.astype(jnp.bfloat16)


def project(offsets, rows, weight, terms):
    count, depth = rows.shape
    width = weight.shape[1]
    block = pick(width, (1024, 256, 128))
    span = terms[0].shape[0]
    return pl.pallas_call(
        functools.partial(project_kernel, len(terms)),
        out_shape=jax.ShapeDtypeStruct((count, width), jnp.bfloat16),
        grid=(width // block,),
        in_specs=[
            pl.BlockSpec(memory_space=pltpu.SMEM),
            pl.BlockSpec((count, depth), lambda j: (0, 0)),
            pl.BlockSpec((depth, block), lambda j: (0, j)),
        ]
        + [pl.BlockSpec((span, block), lambda j: (0, j))] * len(terms),
        out_specs=pl.BlockSpec((count, block), lambda j: (0, j)),
        compiler_params=pltpu.CompilerParams(vmem_limit_bytes=56 << 20),
        cost_estimate=cost(20),
        name="project",
    )(offsets, rows, weight, *terms)


def spread(held, digit):
    ordered = []
    for value in range(len(held)):
        piece = held[0]
        for k in range(1, len(held)):
            piece = jnp.where((digit ^ k) == value, held[k], piece)
        ordered.append(piece)
    return jnp.concatenate(ordered, 0)


def collect(values, axis, size, anchors):
    if size & (size - 1):
        return lax.all_gather(values, axis, axis=0, tiled=False), anchors
    block, step, stage, anchors = values[None], 1, 0, list(anchors)
    while step < size:
        radix = 4 if size // step >= 4 else 2
        held = [block] + [
            lax.ppermute(block, axis, [(i, i ^ (k * step)) for i in range(size)])
            for k in range(1, radix)
        ]
        if stage < len(anchors):
            held, anchors[stage] = lax.optimization_barrier((held, anchors[stage]))
        block = spread(held, lax.axis_index(axis) // step % radix)
        step *= radix
        stage += 1
    return block, anchors


def shards(pops, tps, tokens, norm_gain, weight, pair_seeds, member_ranks):
    owned_rows, width = weight.shape
    pop_index, tp_index = lax.axis_index("pop"), lax.axis_index("tp")
    gathered = lax.all_gather(weight, "pop", axis=0, tiled=True)
    pairs = pair_seeds.shape[0]
    col_start = tp_index * width
    starts = pair_seeds * jnp.int32(mix_seed) + col_start

    span = 2 * ROWS
    if tps == pairs and tokens.shape[0] == span:
        order = [(tp_index + step) % tps for step in range(tps)]
        arrived = [tokens] + [
            lax.ppermute(tokens, "tp", [((i + step) % tps, i) for i in range(tps)])
            for step in range(1, tps)
        ]
    else:
        order = [jnp.int32(step) for step in range(pairs)]
        whole = lax.all_gather(tokens, "tp", axis=0, tiled=True)
        arrived = [whole[i * span : (i + 1) * span] for i in range(pairs)]
    pieces, terms = [], []
    for place, piece in zip(order, arrived):
        if terms:
            piece, terms[-1] = lax.optimization_barrier((piece, terms[-1]))
        pieces.append(normalize(piece, norm_gain))
        start = lax.dynamic_slice(starts, (place,), (1,))
        terms.append(noise_term(start, pieces[-1], width))

    everyone, terms = collect(jnp.concatenate([pair_seeds, member_ranks]), "pop", pops, terms)
    everyone, terms = lax.optimization_barrier((everyone, terms))
    all_seeds = everyone[:, :pairs].reshape(-1)
    all_ranks = everyone[:, pairs:].reshape(-1)
    estimate = make_estimate(
        all_seeds * jnp.int32(mix_seed) + pop_index * (owned_rows * FFW) + col_start,
        all_ranks[0::2] - all_ranks[1::2],
        owned_rows,
        width,
        all_ranks.shape[0],
    )

    offsets = jnp.stack([place * span for place in order]).astype(jnp.int32)
    normed = jnp.concatenate(pieces, 0)
    terms, estimate = lax.optimization_barrier((terms, estimate))
    activated = project(offsets, normed, gathered, terms)
    return (activated, estimate)


def solution(mesh):
    placed = (P(("pop", "tp"), None), P(), P("pop", "tp"), P("pop"), P("pop"))
    return jax.shard_map(
        functools.partial(shards, mesh.shape["pop"], mesh.shape["tp"]),
        mesh=mesh,
        in_specs=placed,
        out_specs=(P("pop", "tp"), P("pop", "tp")),
        check_vma=False,
    )
```
